32 devices in a mesh: gx: 4 (over x, core), gy: 8 (over z, y).
Axes of the slice: x: 2, y: 2, z: 4, core: 2. Of those that a mesh axis runs over, the one named last changes fastest.
Arguments:
- text_feats: bfloat16 [16384, 1152], P(('gx', 'gy')), may hold values from -0.75 to 0.75
- proj: float32 [1152, 1152], P(('gx', 'gy')), may hold values from -0.1875 to 0.1875
- first_moment: float32 [1152, 1152], P(('gx', 'gy')), may hold values from -12 to 12
- second_moment: float32 [1152, 1152], P(('gx', 'gy')), may hold values from 0.1 to 10
- owners: int32 [1024, 5], P(('gx', 'gy')), may hold values from 0 to 31, all different within a row; in each aligned block of 32 rows (0 to 31, 32 to 63, ...) at most 6 rows name the same one
- blocks: int32 [1024, 5], P(('gx', 'gy')), may hold values from 0 to 11
- positives: int32 [16384], P(('gx', 'gy')), may hold values from 0 to 3071
- bank: bfloat16 [98304, 1152], P(('gx', 'gy')), may hold values from -0.1875 to 0.1875
Outputs:
- text_grad: bfloat16 [16384, 1152], P(('gx', 'gy'))
- new_proj: float32 [1152, 1152], P(('gx', 'gy'))
- new_first: float32 [1152, 1152], P(('gx', 'gy'))
- new_second: float32 [1152, 1152], P(('gx', 'gy'))
The draws below stay inside these ranges and needn't reach their ends.
Inputs may be any that keep to these rules, and one draw needn't show every extreme that they name: `owners`: each row names 5 different owner devices, counted in the order gx then gy. Among the text blocks of one device no owner is named more than 6 times, and in some devices' blocks an owner is named exactly 6 times. `positives`: each text row's positive lies in its own device's bank, counted from that device's first bank row.
All inputs are finite; a program needn't handle non-finite values.
Results may differ from the reference program's by a relative error of at most 0.0095.
Values may be sent and summed in bfloat16 or wider, within the bound.
No kernel may reach another device: no remote copies, remote signals or barrier semaphores. Data moves between devices by JAX's collectives and lax.ppermute only.
A program may use at most 128 MiB of HBM per device.

```python
import math
import jax
import jax.numpy as jnp
import numpy as np
from jax import lax

D = 1152
E = 1152
TOK_DEV = 512
BANK_DEV = 3072
TB = 16
BROWS = 256
HARD = 5
TBLK_DEV = 32
NBLK = 12
CAP = 6
TOKENS = 16384
TBLOCKS = 1024
BANK = 98304
N_GX = 4
N_GY = 8


def place_ends(entries, key, smallest, largest):
    longest = entries.shape.index(max(entries.shape))
    spots = []
    for shift in (0, 1):
        where = [jax.random.randint(jax.random.fold_in(key, axis), (), 0, length) for axis, length in enumerate(entries.shape)]
        where[longest] = (where[longest] + shift) % entries.shape[longest]
        spots.append(tuple(where))
    return entries.at[spots[0]].set(smallest).at[spots[1]].set(largest)


def shard_levels(key, shape, shards, least, largest):
    factor_of, own = 1.0, jax.random.fold_in(key, 6)
    for axis_at, parts in shards:
        heights = jnp.exp(jax.random.uniform(jax.random.fold_in(own, axis_at), (parts,), jnp.float32, least / len(shards), largest / len(shards)))
        factor_of = factor_of * jnp.repeat(heights, shape[axis_at] // parts).reshape([-1 if axis == axis_at else 1 for axis in range(len(shape))])
    return factor_of


def routed_block(rng, own, number, rows, number_of, top, most, skew):
    ranking = jax.random.permutation(rng, number_of)
    crowded, common = shares(number_of, rows * top, most, skew, True), shares(number_of, rows * top, most, skew, False)
    places = jnp.arange(number_of)

    def named(tallies, turn):
        used = int((tallies > 0).sum())
        fixed = max(1, used // 4)
        shifted = fixed + (places - fixed + turn * (used - fixed)) % max(1, number_of - fixed)
        return jnp.zeros((number_of,), jnp.int32).at[ranking[jnp.where(places < fixed, places, shifted)]].set(jnp.asarray(tallies, jnp.int32))

    tallies = jnp.where(number % 4 == 0, named(crowded, number // 4), named(common, number - number // 4 - 1))
    mixed = jax.random.permutation(jax.random.fold_in(own, 3), number_of)
    donor, sink = mixed[0:number_of // 2 * 2:2], mixed[1:number_of // 2 * 2:2]
    room = jnp.minimum(tallies[donor] - 1, most - tallies[sink]) // 2
    room = jnp.where((donor == ranking[0]) | (sink == ranking[0]) | (tallies[sink] == 0), 0, jnp.maximum(room, 0))
    shifted = jax.random.randint(jax.random.fold_in(own, 4), (number_of // 2,), 0, 1 << 20) % (room + 1)
    tallies = tallies.at[donor].add(-shifted).at[sink].add(shifted)
    items = jnp.searchsorted(jnp.cumsum(tallies), jnp.arange(rows * top), side="right").astype(jnp.int32)
    listing = items.reshape(top, rows).T
    listing = listing[jax.random.permutation(jax.random.fold_in(own, 1), rows)]
    turn = jax.random.randint(jax.random.fold_in(own, 2), (rows, 1), 0, top)
    return jnp.take_along_axis(listing, (jnp.arange(top)[None, :] + turn) % top, axis=1)


def shares(number_of, total, bound, lean, full):
    loads = [(1 << 20) // math.isqrt(grade ** lean) + 1 for grade in range(1, number_of + 1)]
    largest = bound if full else min(bound, max(-(-total // number_of), total * loads[0] // sum(loads)))
    least = 1 if total - largest >= number_of - 1 else 0
    holding, surplus = [largest] + [least] * (number_of - 1), total - largest - least * (number_of - 1)
    while surplus > 0:
        movable = [i for i in range(1, number_of) if holding[i] < largest] or [i for i in range(1, number_of) if holding[i] < bound]
        mass, left = sum([loads[i] for i in movable]), surplus
        for i in movable:
            extra = min(bound - holding[i], max(1, left * loads[i] // mass), surplus)
            holding[i] = holding[i] + extra
            surplus = surplus - extra
    return np.array(holding)


def centred(rng, shape, width, most, cuts=(), held_as=jnp.bfloat16):
    gain = shard_levels(rng, shape, cuts, -0.22, 0.18) if cuts else 1.0
    entries = jax.random.normal(rng, shape, jnp.float32) * width * gain
    return jnp.minimum(jnp.maximum(entries, -most), most).astype(held_as)


def setup_inputs(seed: int = 0) -> dict:
    key_of = jax.random.split(jax.random.key(seed), 9)
    text_feats = centred(key_of[0], (TOKENS, D), 0.125, 0.75, ((0, 32),))
    proj = centred(key_of[1], (D, E), D ** -0.5, 0.1875, ((0, 32),), jnp.float32)
    first_moment = centred(key_of[2], (D, E), 2.0, 12.0, ((0, 32),), jnp.float32)
    second_moment = jnp.clip(jnp.exp(math.log(10.0) - 4.6051702 * jax.random.uniform(key_of[3], (D, E), jnp.float32) ** shard_levels(key_of[3], (D, E), ((0, 32),), -0.2, 0.2)), 0.1, 10.0)
    owners_keys = jax.random.split(jax.random.fold_in(key_of[4], 1), TBLOCKS // TBLK_DEV)
    owners_turns = jax.random.permutation(jax.random.fold_in(key_of[4], 3), TBLOCKS // TBLK_DEV)
    owners = jax.vmap(lambda own, number: routed_block(jax.random.fold_in(key_of[4], 2), own, number, TBLK_DEV, N_GX * N_GY, HARD, CAP, 2))(owners_keys, owners_turns).reshape((TBLOCKS, HARD))
    blocks = place_ends(jax.random.randint(key_of[5], (TBLOCKS, HARD), 0, NBLK), jax.random.fold_in(key_of[5], 1), 0, NBLK - 1).astype(jnp.int32)
    positives = place_ends(jax.random.randint(key_of[6], (TOKENS,), 0, BANK_DEV), jax.random.fold_in(key_of[6], 1), 0, BANK_DEV - 1).astype(jnp.int32)
    bank = centred(key_of[7], (BANK, E), E ** -0.5, 0.1875, ((0, 32),))
    return dict(text_feats=text_feats, proj=proj, first_moment=first_moment, second_moment=second_moment, owners=owners, blocks=blocks, positives=positives, bank=bank)


logit_scale = 20.0
logit_bias = -3.0
norm_eps = 1e-06
beta_one = 0.9
beta_two = 0.999
learn_rate = 0.001
decay_rate = 0.1
adam_eps = 1e-08
adam_step = 100.0

def reference(text_feats, proj, first_moment, second_moment, owners, blocks, positives, bank):
    device_count = N_GX * N_GY
    weight_half = proj.astype(jnp.bfloat16)
    projected = jnp.dot(text_feats, weight_half, preferred_element_type=jnp.float32)
    radius = jnp.sqrt(lax.optimization_barrier(jnp.sum(projected * projected, axis=-1, keepdims=True)) + norm_eps)
    unit_rows = projected / radius
    unit_half = unit_rows.astype(jnp.bfloat16)
    bank_local = bank.reshape(device_count, BANK_DEV, E)
    bank_blocks = bank.reshape(device_count * NBLK, BROWS, E)
    text_dev = unit_half.reshape(device_count, TOK_DEV, E)
    pos_dev = positives.reshape(device_count, TOK_DEV)
    own_dev = owners.reshape(device_count, TBLK_DEV, HARD)
    blk_dev = blocks.reshape(device_count, TBLK_DEV, HARD)

    def one_device(pieces):
        text_rows, local_bank, positive_ids, owner_ids, block_ids = pieces
        scores = logit_scale * jnp.dot(text_rows, local_bank.T, preferred_element_type=jnp.float32) + logit_bias
        columns = jnp.arange(BANK_DEV, dtype=jnp.int32)
        labels = jnp.where(columns[None, :] == positive_ids[:, None], 1.0, -1.0).astype(jnp.float32)
        local_coef = (-labels * jax.nn.sigmoid(-labels * scores)).astype(jnp.bfloat16)
        local_grad = logit_scale * jnp.dot(local_coef, local_bank, preferred_element_type=jnp.float32)
        global_ids = (owner_ids * NBLK + block_ids).astype(jnp.int32)
        picked = bank_blocks[global_ids].astype(jnp.float32)
        block_rows = text_rows.reshape(TBLK_DEV, TB, E).astype(jnp.float32)
        hard_scores = logit_scale * jnp.einsum('kte,kvbe->kvtb', block_rows, picked) + logit_bias
        hard_coef = jax.nn.sigmoid(hard_scores).astype(jnp.bfloat16)
        per_visit = (logit_scale * jnp.einsum('kvtb,kvbe->kvte', hard_coef.astype(jnp.float32), picked)).astype(jnp.bfloat16)
        visit_sum = lax.optimization_barrier(jnp.sum(per_visit.astype(jnp.float32), axis=1)).reshape(TOK_DEV, E)
        return local_grad + visit_sum
    embed_grad = lax.map(one_device, (text_dev, bank_local, pos_dev, own_dev, blk_dev)).reshape(TOKENS, E)
    radial = lax.optimization_barrier(jnp.sum(unit_rows * embed_grad, axis=-1, keepdims=True))
    proj_grad_rows = ((embed_grad - unit_rows * radial) / radius).astype(jnp.bfloat16)
    text_grad = jnp.dot(proj_grad_rows, weight_half.T, preferred_element_type=jnp.float32).astype(jnp.bfloat16)
    weight_grad = jnp.dot(text_feats.T, proj_grad_rows, preferred_element_type=jnp.float32)
    new_first = beta_one * first_moment + (1.0 - beta_one) * weight_grad
    new_second = beta_two * second_moment + (1.0 - beta_two) * weight_grad * weight_grad
    first_hat = new_first / (1.0 - beta_one ** adam_step)
    second_hat = new_second / (1.0 - beta_two ** adam_step)
    new_proj = proj - learn_rate * (first_hat / (jnp.sqrt(second_hat) + adam_eps) + decay_rate * proj)
    return (text_grad, new_proj, new_first, new_second)
```

```python
import functools

import jax
import jax.numpy as jnp
from jax import lax
from jax.experimental import pallas as pl
from jax.experimental.pallas import tpu as pltpu
from jax.sharding import Mesh, PartitionSpec as P

BROWS = 256
TILE_SLOTS = 8

logit_scale = 20.0
logit_bias = -3.0
norm_eps = 1e-06
beta_one = 0.9
beta_two = 0.999
learn_rate = 0.001
decay_rate = 0.1
adam_eps = 1e-08
adam_step = 100.0

ALL = ("x", "c", "zh", "zl", "y")
PLANE = ("x", "c", "y")
COLUMN = ("zh", "zl")
SWAP = [(0, 1), (1, 0)]
bf16 = jnp.bfloat16
f32 = jnp.float32


def answer_kernel(
    slots, tb, banks, row_chunk, tags_ref, x_ref, w_hbm, bank_hbm, out_ref,
    w_ref, bank_ref, unit_ref, order_ref, count_ref, tile_bank, tile_first, tile_last, sems,
):
    w_copy = pltpu.make_async_copy(w_hbm, w_ref, sems.at[0])
    bank_copy = pltpu.make_async_copy(bank_hbm, bank_ref, sems.at[1])
    w_copy.start()
    bank_copy.start()

    for b in range(banks):
        count_ref[b] = 0

    def count(s, carry):
        b = tags_ref[s]
        count_ref[b] = count_ref[b] + 1
        return carry

    lax.fori_loop(0, slots, count, 0)

    def lay(b, carry):
        first, tiles = carry
        n = count_ref[b]
        last = first + n - 1

        def tile(i, carry):
            tile_bank[tiles + i] = b
            tile_first[tiles + i] = first + i * TILE_SLOTS
            tile_last[tiles + i] = last
            return carry

        n_tiles = lax.div(n + TILE_SLOTS - 1, TILE_SLOTS)
        lax.fori_loop(0, n_tiles, tile, 0)
        count_ref[b] = first
        return first + n, tiles + n_tiles

    _, n_tiles = lax.fori_loop(0, banks, lay, (0, 0))

    def place(s, carry):
        b = tags_ref[s]
        at = count_ref[b]
        order_ref[at] = s
        count_ref[b] = at + 1
        return carry

    lax.fori_loop(0, slots, place, 0)

    w_copy.wait()

    def project(i, carry):
        rows = pl.ds(pl.multiple_of(i * row_chunk, row_chunk), row_chunk)
        projected = jnp.dot(x_ref[rows, :], w_ref[...], preferred_element_type=f32)
        radius = jnp.sqrt(jnp.sum(projected * projected, axis=-1, keepdims=True) + norm_eps)
        unit_ref[rows, :] = (projected * (1.0 / radius)).astype(bf16)
        return carry

    lax.fori_loop(0, slots * tb // row_chunk, project, 0)
    bank_copy.wait()

    def answer(t, carry):
        b = tile_bank[t]
        first = tile_first[t]
        last = tile_last[t]
        at = []
        for i in range(TILE_SLOTS):
            at.append(pl.multiple_of(order_ref[jnp.minimum(first + i, last)] * tb, tb))
        queries = jnp.concatenate([unit_ref[pl.ds(a, tb), :] for a in at], axis=0)
        keys = bank_ref[pl.ds(pl.multiple_of(b * BROWS, BROWS), BROWS), :]
        scores = lax.dot_general(queries, keys, (((1,), (1,)), ((), ())), preferred_element_type=f32)
        coef = jax.nn.sigmoid(logit_scale * scores + logit_bias).astype(bf16)
        grad = logit_scale * jnp.dot(coef, keys, preferred_element_type=f32)
        grad = grad.astype(bf16)
        for i, a in enumerate(at):
            out_ref[pl.ds(a, tb), :] = grad[i * tb : (i + 1) * tb, :]
        return carry

    lax.fori_loop(0, n_tiles, answer, 0)


def answer(x, tags, weight_half, bank, tb):
    rows, width = x.shape
    slots = rows // tb
    banks = bank.shape[0] // BROWS
    most_tiles = slots // TILE_SLOTS + banks + 1
    row_chunk = 256 if rows % 256 == 0 else tb
    return pl.pallas_call(
        functools.partial(answer_kernel, slots, tb, banks, row_chunk),
        out_shape=jax.ShapeDtypeStruct((rows, bank.shape[1]), bf16),
        in_specs=[
            pl.BlockSpec(memory_space=pltpu.SMEM),
            pl.BlockSpec(memory_space=pltpu.VMEM),
            pl.BlockSpec(memory_space=pl.ANY),
            pl.BlockSpec(memory_space=pl.ANY),
        ],
        out_specs=pl.BlockSpec(memory_space=pltpu.VMEM),
        scratch_shapes=[
            pltpu.VMEM(weight_half.shape, bf16),
            pltpu.VMEM(bank.shape, bf16),
            pltpu.VMEM((rows, bank.shape[1]), bf16),
            pltpu.SMEM((slots,), jnp.int32),
            pltpu.SMEM((banks,), jnp.int32),
            pltpu.SMEM((most_tiles,), jnp.int32),
            pltpu.SMEM((most_tiles,), jnp.int32),
            pltpu.SMEM((most_tiles,), jnp.int32),
            pltpu.SemaphoreType.DMA((2,)),
        ],
        compiler_params=pltpu.CompilerParams(vmem_limit_bytes=40 << 20),
        cost_estimate=pl.CostEstimate(
            flops=2 * rows * width * width + 8 * rows * width * BROWS,
            bytes_accessed=4 * rows * width + 2 * width * width + 2 * bank.size,
            transcendentals=rows * BROWS,
        ),
        name="answer",
    )(tags, x, weight_half, bank)


def route(owners, blocks, capacity, tb):
    n_blocks, hard = owners.shape
    visits = n_blocks * hard
    n_x, n_c, n_h, n_l, n_y = (lax.axis_size(a) for a in ALL)
    x, c, zh, zl, y = (lax.axis_index(a) for a in ALL)
    devices = n_x * n_c * n_h * n_l * n_y
    pad = -(2 * visits) % 1024
    own = jnp.concatenate([owners.reshape(-1), blocks.reshape(-1), jnp.zeros((pad,), jnp.int32)])
    table = jnp.broadcast_to(own.reshape(1, -1, 128), (devices, own.shape[0] // 128, 128))
    table = lax.all_to_all(table, ALL, split_axis=0, concat_axis=0, tiled=True)
    table = table.reshape(n_x, n_c, n_h, n_l, n_y, -1)
    table = jnp.where(zh == 0, table, jnp.flip(table, 2))
    table = jnp.where(zl == 0, table, jnp.flip(table, 3))
    table = table.transpose(2, 3, 0, 1, 4, 5).reshape(n_h * n_l, n_x * n_c * n_y, -1)
    plane_at = (x * n_c + c) * n_y + y
    mine = lax.dynamic_index_in_dim(table, plane_at, 1, keepdims=False)[:, None, :visits]
    xs, cs, ys = jnp.arange(n_x), jnp.arange(n_c), jnp.arange(n_y)
    z_at = zh * n_l + zl
    dest = (((xs[:, None, None] * n_c + cs[None, :, None]) * (n_h * n_l)) + z_at) * n_y + ys[None, None, :]
    me = ((x * n_c + c) * (n_h * n_l) + z_at) * n_y + y
    sent = mine == dest.reshape(1, -1, 1)
    got = table[:, :, :visits] == me
    both = jnp.stack([sent, got])
    order = jnp.arange(visits, dtype=jnp.int32)
    before = (order[:, None] < order[None, :]).astype(bf16)
    rank = jnp.dot(both.astype(bf16), before, preferred_element_type=f32)
    values = jnp.stack([jnp.broadcast_to(order // hard + 1, got.shape), table[:, :, visits : 2 * visits] + 1])
    hit = both[..., None, :] & (rank[..., None, :] == jnp.arange(capacity, dtype=f32)[:, None])
    picked = jnp.sum(jnp.where(hit, values[..., None, :], 0), axis=-1) - 1
    picked = picked.reshape(2, n_h * n_l, -1)
    return picked[0], jnp.maximum(picked[1], 0)


def gather_weight(proj):
    n_x, n_c, n_h, n_l, n_y = (lax.axis_size(a) for a in ALL)
    rows, width = proj.shape
    piece = proj.astype(bf16)[None]
    n_z = n_h * n_l
    piece = lax.all_to_all(jnp.broadcast_to(piece, (n_z, rows, width)), COLUMN, split_axis=0, concat_axis=0, tiled=True)
    piece = jnp.broadcast_to(piece[None], (n_x * n_y, n_z, rows, width))
    piece = lax.all_to_all(piece, ("x", "y"), split_axis=0, concat_axis=0, tiled=True)
    other = lax.ppermute(piece, "c", SWAP)
    low = lax.axis_index("c") == 0
    both = jnp.stack([jnp.where(low, piece, other), jnp.where(low, other, piece)])
    both = both.reshape(n_c, n_x, n_y, n_z, rows, width).transpose(1, 0, 3, 2, 4, 5)
    return both.reshape(-1, width)


def reduce_weight(grad):
    n_x, n_c, n_h, n_l, n_y = (lax.axis_size(a) for a in ALL)
    width = grad.shape[1]
    n_z = n_h * n_l
    rows = grad.shape[0] // (n_x * n_c * n_z * n_y)
    grad = grad.reshape(n_x, n_c, n_z * n_y * rows, width)
    c = lax.axis_index("c")
    send = lax.dynamic_index_in_dim(grad, 1 - c, 1, keepdims=False).astype(bf16)
    keep = lax.dynamic_index_in_dim(grad, c, 1, keepdims=False)
    total = keep + lax.ppermute(send, "c", SWAP).astype(f32)
    total = total.reshape(n_x, n_z, n_y, rows, width).transpose(0, 2, 1, 3, 4)
    total = total.reshape(n_x * n_y, n_z * rows, width).astype(bf16)
    total = lax.all_to_all(total, ("x", "y"), split_axis=0, concat_axis=0, tiled=True)
    total = jnp.sum(total.astype(f32), axis=0).reshape(n_z, rows, width).astype(bf16)
    total = lax.all_to_all(total, COLUMN, split_axis=0, concat_axis=0, tiled=True)
    return jnp.sum(total.astype(f32), axis=0)


def local(text_feats, proj, first_moment, second_moment, owners, blocks, positives, bank):
    devices = lax.axis_size(ALL)
    plane = lax.axis_size(PLANE)
    rows_dev, width = text_feats.shape
    text_blocks, hard = owners.shape
    tb = rows_dev // text_blocks
    visits = text_blocks * hard
    capacity = max(2, visits // devices + 1)
    embed_width = bank.shape[1]

    text_low = lax.ppermute(text_feats, "zl", SWAP)
    text_high = lax.ppermute(text_feats, "zh", SWAP)
    text_far = lax.ppermute(text_high, "zl", SWAP)
    texts = (text_feats, text_low, text_high, text_far)
    sources, tags = route(owners, blocks, capacity, tb)
    weight_half = gather_weight(proj)

    def exchange(rows):
        rows = rows.reshape(plane, capacity * tb, -1)
        rows = lax.all_to_all(rows, PLANE, split_axis=0, concat_axis=0, tiled=True)
        return rows.reshape(plane * capacity * tb, -1)

    partial = []
    for k in range(4):
        row_of = sources[k][:, None] * tb + jnp.arange(tb, dtype=jnp.int32)[None, :]
        row_of = jnp.where(sources[k][:, None] >= 0, row_of, -1).reshape(-1)
        pick = (row_of[:, None] == jnp.arange(rows_dev, dtype=jnp.int32)[None, :]).astype(bf16)
        sent = jnp.dot(pick, texts[k], preferred_element_type=f32).astype(bf16)
        replies = exchange(answer(exchange(sent), tags[k], weight_half, bank, tb))
        partial.append(
            lax.dot_general(pick, replies, (((0,), (0,)), ((), ())), preferred_element_type=f32)
        )
    from_far = lax.ppermute(partial[3].astype(bf16), "zl", SWAP)
    from_high = lax.ppermute((partial[2] + from_far.astype(f32)).astype(bf16), "zh", SWAP)
    from_low = lax.ppermute(partial[1].astype(bf16), "zl", SWAP)
    visit_sum = partial[0] + from_low.astype(f32) + from_high.astype(f32)

    projected = jnp.dot(text_feats, weight_half, preferred_element_type=f32)
    radius = jnp.sqrt(jnp.sum(projected * projected, axis=-1, keepdims=True) + norm_eps)
    unit_rows = projected / radius
    unit_half = unit_rows.astype(bf16)
    scores = logit_scale * jnp.dot(unit_half, bank.T, preferred_element_type=f32) + logit_bias
    columns = jnp.arange(bank.shape[0], dtype=jnp.int32)
    labels = jnp.where(columns[None, :] == positives[:, None], 1.0, -1.0).astype(f32)
    local_coef = (-labels * jax.nn.sigmoid(-labels * scores)).astype(bf16)
    local_grad = logit_scale * jnp.dot(local_coef, bank, preferred_element_type=f32)

    embed_grad = local_grad + visit_sum
    radial = jnp.sum(unit_rows * embed_grad, axis=-1, keepdims=True)
    proj_grad_rows = ((embed_grad - unit_rows * radial) / radius).astype(bf16)
    weight_grad = reduce_weight(
        lax.dot_general(text_feats, proj_grad_rows, (((0,), (0,)), ((), ())), preferred_element_type=f32)
    )
    text_grad = jnp.dot(proj_grad_rows, weight_half.T, preferred_element_type=f32).astype(bf16)
    new_first = beta_one * first_moment + (1.0 - beta_one) * weight_grad
    new_second = beta_two * second_moment + (1.0 - beta_two) * weight_grad * weight_grad
    first_hat = new_first / (1.0 - beta_one**adam_step)
    second_hat = new_second / (1.0 - beta_two**adam_step)
    new_proj = proj - learn_rate * (first_hat / (jnp.sqrt(second_hat) + adam_eps) + decay_rate * proj)
    return (text_grad, new_proj, new_first, new_second)


def solution(mesh):
    n_gx, n_gy = mesh.shape["gx"], mesh.shape["gy"]
    fine = Mesh(mesh.devices.reshape(n_gx // 2, 2, 2, 2, n_gy // 4), ALL)
    rows = P(ALL, None)
    return jax.shard_map(
        local,
        mesh=fine,
        in_specs=(rows, rows, rows, rows, rows, rows, P(ALL), rows),
        out_specs=(rows, rows, rows, rows),
        check_vma=False,
    )
```

```python
import functools

import jax
import jax.numpy as jnp
from jax import lax
from jax.experimental import pallas as pl
from jax.experimental.pallas import tpu as pltpu
from jax.sharding import Mesh, PartitionSpec as P


BROWS = 256
TILE_SLOTS = 8

logit_scale = 20.0
logit_bias = -3.0
norm_eps = 1e-06
beta_one = 0.9
beta_two = 0.999
learn_rate = 0.001
decay_rate = 0.1
adam_eps = 1e-08
adam_step = 100.0

ALL = ("x", "c", "zh", "zl", "y")
PLANE = ("x", "c", "y")
COLUMN = ("zh", "zl")
SWAP = [(0, 1), (1, 0)]
bf16 = jnp.bfloat16
f32 = jnp.float32


def answer_kernel(
    slots, tb, banks, row_chunk, tags_ref, x_ref, w_ref, bank_hbm, out_ref,
    bank_ref, unit_ref, order_ref, count_ref, tile_bank, tile_first, tile_last, sem,
):
    bank_copy = pltpu.make_async_copy(bank_hbm, bank_ref, sem)
    bank_copy.start()

    for b in range(banks):
        count_ref[b] = 0

    def count(s, carry):
        b = tags_ref[s]
        count_ref[b] = count_ref[b] + 1
        return carry

    lax.fori_loop(0, slots, count, 0)

    def lay(b, carry):
        first, tiles = carry
        n = count_ref[b]
        last = first + n - 1

        def tile(i, carry):
            tile_bank[tiles + i] = b
            tile_first[tiles + i] = first + i * TILE_SLOTS
            tile_last[tiles + i] = last
            return carry

        n_tiles = lax.div(n + TILE_SLOTS - 1, TILE_SLOTS)
        lax.fori_loop(0, n_tiles, tile, 0)
        count_ref[b] = first
        return first + n, tiles + n_tiles

    _, n_tiles = lax.fori_loop(0, banks, lay, (0, 0))

    def place(s, carry):
        b = tags_ref[s]
        at = count_ref[b]
        order_ref[at] = s
        count_ref[b] = at + 1
        return carry

    lax.fori_loop(0, slots, place, 0)

    def project(i, carry):
        rows = pl.ds(pl.multiple_of(i * row_chunk, row_chunk), row_chunk)
        projected = jnp.dot(x_ref[rows, :], w_ref[...], preferred_element_type=f32)
        radius = jnp.sqrt(jnp.sum(projected * projected, axis=-1, keepdims=True) + norm_eps)
        unit_ref[rows, :] = (projected * (1.0 / radius)).astype(bf16)
        return carry

    lax.fori_loop(0, slots * tb // row_chunk, project, 0)
    bank_copy.wait()

    def answer(t, carry):
        b = tile_bank[t]
        first = tile_first[t]
        last = tile_last[t]
        at = []
        for i in range(TILE_SLOTS):
            at.append(pl.multiple_of(order_ref[jnp.minimum(first + i, last)] * tb, tb))
        queries = jnp.concatenate([unit_ref[pl.ds(a, tb), :] for a in at], axis=0)
        keys = bank_ref[pl.ds(pl.multiple_of(b * BROWS, BROWS), BROWS), :]
        scores = lax.dot_general(queries, keys, (((1,), (1,)), ((), ())), preferred_element_type=f32)
        coef = jax.nn.sigmoid(logit_scale * scores + logit_bias).astype(bf16)
        grad = logit_scale * jnp.dot(coef, keys, preferred_element_type=f32)
        grad = grad.astype(bf16)
        for i, a in enumerate(at):
            out_ref[pl.ds(a, tb), :] = grad[i * tb : (i + 1) * tb, :]
        return carry

    lax.fori_loop(0, n_tiles, answer, 0)


def answer(x, tags, weight_half, bank, tb):
    rows, width = x.shape
    slots = rows // tb
    banks = bank.shape[0] // BROWS
    most_tiles = slots // TILE_SLOTS + banks + 1
    row_chunk = 128 if rows % 128 == 0 else tb
    return pl.pallas_call(
        functools.partial(answer_kernel, slots, tb, banks, row_chunk),
        out_shape=jax.ShapeDtypeStruct((rows, bank.shape[1]), bf16),
        in_specs=[
            pl.BlockSpec(memory_space=pltpu.SMEM),
            pl.BlockSpec(memory_space=pltpu.VMEM),
            pl.BlockSpec(memory_space=pltpu.VMEM),
            pl.BlockSpec(memory_space=pltpu.HBM),
        ],
        out_specs=pl.BlockSpec(memory_space=pltpu.VMEM),
        scratch_shapes=[
            pltpu.VMEM(bank.shape, bf16),
            pltpu.VMEM((rows, bank.shape[1]), bf16),
            pltpu.SMEM((slots,), jnp.int32),
            pltpu.SMEM((banks,), jnp.int32),
            pltpu.SMEM((most_tiles,), jnp.int32),
            pltpu.SMEM((most_tiles,), jnp.int32),
            pltpu.SMEM((most_tiles,), jnp.int32),
            pltpu.SemaphoreType.DMA,
        ],
        compiler_params=pltpu.CompilerParams(vmem_limit_bytes=40 << 20),
        cost_estimate=pl.CostEstimate(
            flops=2 * rows * width * width + 8 * rows * width * BROWS,
            bytes_accessed=4 * rows * width + 2 * width * width + 2 * bank.size,
            transcendentals=rows * BROWS,
        ),
        name="answer",
    )(tags, x, weight_half, bank)


def route(owners, blocks, capacity):
    n_blocks, hard = owners.shape
    visits = n_blocks * hard
    n_x, n_c, n_h, n_l, n_y = (lax.axis_size(a) for a in ALL)
    x, c, zh, zl, y = (lax.axis_index(a) for a in ALL)
    devices = n_x * n_c * n_h * n_l * n_y
    pad = -(2 * visits) % 1024
    own = jnp.concatenate([owners.reshape(-1), blocks.reshape(-1), jnp.zeros((pad,), jnp.int32)])
    table = jnp.broadcast_to(own.reshape(1, -1, 128), (devices, own.shape[0] // 128, 128))
    table = lax.all_to_all(table, ALL, split_axis=0, concat_axis=0, tiled=True)
    table = table.reshape(n_x, n_c, n_h, n_l, n_y, -1)
    table = jnp.where(zh == 0, table, jnp.flip(table, 2))
    table = jnp.where(zl == 0, table, jnp.flip(table, 3))
    table = table.transpose(2, 3, 0, 1, 4, 5).reshape(n_h * n_l, n_x * n_c * n_y, -1)
    plane_at = (x * n_c + c) * n_y + y
    mine = lax.dynamic_index_in_dim(table, plane_at, 1, keepdims=False)[:, None, :visits]
    xs, cs, ys = jnp.arange(n_x), jnp.arange(n_c), jnp.arange(n_y)
    z_at = zh * n_l + zl
    dest = (((xs[:, None, None] * n_c + cs[None, :, None]) * (n_h * n_l)) + z_at) * n_y + ys[None, None, :]
    me = ((x * n_c + c) * (n_h * n_l) + z_at) * n_y + y
    sent = mine == dest.reshape(1, -1, 1)
    got = table[:, :, :visits] == me
    both = jnp.stack([sent, got])
    order = jnp.arange(visits, dtype=jnp.int32)
    before = (order[:, None] < order[None, :]).astype(bf16)
    rank = jnp.dot(both.astype(bf16), before, preferred_element_type=f32)
    values = jnp.stack([jnp.broadcast_to(order // hard + 1, got.shape), table[:, :, visits : 2 * visits] + 1])
    hit = both[..., None, :] & (rank[..., None, :] == jnp.arange(capacity, dtype=f32)[:, None])
    picked = jnp.sum(jnp.where(hit, values[..., None, :], 0), axis=-1) - 1
    picked = picked.reshape(2, n_h * n_l, -1)
    return picked[0], jnp.maximum(picked[1], 0)


def gather_weight(proj):
    n_x, n_c, n_h, n_l, n_y = (lax.axis_size(a) for a in ALL)
    x, c, zh, zl, y = (lax.axis_index(a) for a in ALL)
    rows, width = proj.shape
    n_z, n_xy = n_h * n_l, n_x * n_y
    piece = jnp.pad(proj.astype(bf16), ((0, -rows % 8), (0, 0)))[None]
    column = [piece]
    for k in range(1, n_z):
        column.append(lax.ppermute(piece, COLUMN, [(i, i ^ k) for i in range(n_z)]))
    piece = jnp.concatenate(column)
    flat = [piece]
    for k in range(1, n_xy):
        flat.append(lax.ppermute(piece, ("x", "y"), [(i, i ^ k) for i in range(n_xy)]))
    piece = jnp.concatenate(flat)
    other = lax.ppermute(piece, "c", SWAP)
    piece = jnp.concatenate([piece, other])
    xs, cs, zs, ys = jnp.arange(n_x), jnp.arange(n_c), jnp.arange(n_z), jnp.arange(n_y)
    far_c = (cs ^ c)[None, :, None, None]
    far_xy = ((xs[:, None] * n_y + ys[None, :]) ^ (x * n_y + y))[:, None, None, :]
    far_z = (zs ^ (zh * n_l + zl))[None, None, :, None]
    at = ((far_c * n_xy + far_xy) * n_z + far_z).reshape(-1)
    return jnp.take(piece, at, axis=0)[:, :rows].reshape(-1, width)


def reduce_weight(grad):
    n_x, n_c, n_h, n_l, n_y = (lax.axis_size(a) for a in ALL)
    width = grad.shape[1]
    n_z = n_h * n_l
    rows = grad.shape[0] // (n_x * n_c * n_z * n_y)
    grad = grad.reshape(n_x, n_c, n_z * n_y * rows, width)
    c = lax.axis_index("c")
    send = lax.dynamic_index_in_dim(grad, 1 - c, 1, keepdims=False).astype(bf16)
    keep = lax.dynamic_index_in_dim(grad, c, 1, keepdims=False)
    total = keep + lax.ppermute(send, "c", SWAP).astype(f32)
    total = total.reshape(n_x, n_z, n_y, rows, width).transpose(0, 2, 1, 3, 4)
    total = total.reshape(n_x * n_y, n_z * rows, width).astype(bf16)
    total = lax.all_to_all(total, ("x", "y"), split_axis=0, concat_axis=0, tiled=True)
    total = jnp.sum(total.astype(f32), axis=0).reshape(n_z, rows, width).astype(bf16)
    total = lax.all_to_all(total, COLUMN, split_axis=0, concat_axis=0, tiled=True)
    return jnp.sum(total.astype(f32), axis=0)


def step(text_feats, proj, first_moment, second_moment, owners, blocks, positives, bank):
    devices = lax.axis_size(ALL)
    plane = lax.axis_size(PLANE)
    rows_dev, _ = text_feats.shape
    text_blocks, hard = owners.shape
    tb = rows_dev // text_blocks
    visits = text_blocks * hard
    capacity = max(2, visits // devices + 1)

    text_high = lax.ppermute(text_feats, "zh", SWAP)
    text_low = lax.ppermute(text_feats, "zl", SWAP)
    text_far = lax.ppermute(text_high, "zl", SWAP)
    texts = (text_feats, text_low, text_high, text_far)
    sources, tags = route(owners, blocks, capacity)
    weight_half = gather_weight(proj)

    def exchange(rows):
        rows = rows.reshape(plane, capacity * tb, -1)
        rows = lax.all_to_all(rows, PLANE, split_axis=0, concat_axis=0, tiled=True)
        return rows.reshape(plane * capacity * tb, -1)

    partial = []
    for k in range(4):
        row_of = sources[k][:, None] * tb + jnp.arange(tb, dtype=jnp.int32)[None, :]
        row_of = jnp.where(sources[k][:, None] >= 0, row_of, -1).reshape(-1)
        pick = (row_of[:, None] == jnp.arange(rows_dev, dtype=jnp.int32)[None, :]).astype(bf16)
        sent = jnp.dot(pick, texts[k], preferred_element_type=f32).astype(bf16)
        got = exchange(sent)
        replies = answer(got, tags[k], weight_half, bank, tb)
        replies = exchange(replies)
        partial.append(
            lax.dot_general(pick, replies, (((0,), (0,)), ((), ())), preferred_element_type=f32)
        )
    from_far = lax.ppermute(partial[3].astype(bf16), "zl", SWAP)
    from_high = lax.ppermute((partial[2] + from_far.astype(f32)).astype(bf16), "zh", SWAP)
    from_low = lax.ppermute(partial[1].astype(bf16), "zl", SWAP)
    visit_sum = partial[0] + from_low.astype(f32) + from_high.astype(f32)

    projected = jnp.dot(text_feats, weight_half, preferred_element_type=f32)
    radius = jnp.sqrt(jnp.sum(projected * projected, axis=-1, keepdims=True) + norm_eps)
    unit_rows = projected / radius
    unit_half = unit_rows.astype(bf16)
    scores = logit_scale * jnp.dot(unit_half, bank.T, preferred_element_type=f32) + logit_bias
    columns = jnp.arange(bank.shape[0], dtype=jnp.int32)
    labels = jnp.where(columns[None, :] == positives[:, None], 1.0, -1.0).astype(f32)
    local_coef = (-labels * jax.nn.sigmoid(-labels * scores)).astype(bf16)
    local_grad = logit_scale * jnp.dot(local_coef, bank, preferred_element_type=f32)
    local_grad, unit_rows, radius = lax.optimization_barrier((local_grad, unit_rows, radius))

    embed_grad = local_grad + visit_sum
    radial = jnp.sum(unit_rows * embed_grad, axis=-1, keepdims=True)
    proj_grad_rows = ((embed_grad - unit_rows * radial) / radius).astype(bf16)
    weight_grad = reduce_weight(
        lax.dot_general(text_feats, proj_grad_rows, (((0,), (0,)), ((), ())), preferred_element_type=f32)
    )
    text_grad = jnp.dot(proj_grad_rows, weight_half.T, preferred_element_type=f32).astype(bf16)
    new_first = beta_one * first_moment + (1.0 - beta_one) * weight_grad
    new_second = beta_two * second_moment + (1.0 - beta_two) * weight_grad * weight_grad
    first_hat = new_first / (1.0 - beta_one**adam_step)
    second_hat = new_second / (1.0 - beta_two**adam_step)
    new_proj = proj - learn_rate * (first_hat / (jnp.sqrt(second_hat) + adam_eps) + decay_rate * proj)
    return (text_grad, new_proj, new_first, new_second)


def solution(mesh):
    n_gx, n_gy = mesh.shape["gx"], mesh.shape["gy"]
    fine = Mesh(mesh.devices.reshape(n_gx // 2, 2, 2, 2, n_gy // 4), ALL)
    rows = P(ALL, None)
    return jax.shard_map(
        step,
        mesh=fine,
        in_specs=(rows, rows, rows, rows, rows, rows, P(ALL), rows),
        out_specs=(rows, rows, rows, rows),
        check_vma=False,
    )
```

```python
import functools

import jax
import jax.numpy as jnp
from jax import lax
from jax.experimental import pallas as pl
from jax.experimental.pallas import tpu as pltpu
from jax.sharding import Mesh, PartitionSpec as P


BROWS = 256
TILE_SLOTS = 8

logit_scale = 20.0
logit_bias = -3.0
norm_eps = 1e-06
beta_one = 0.9
beta_two = 0.999
learn_rate = 0.001
decay_rate = 0.1
adam_eps = 1e-08
adam_step = 100.0

ALL = ("x", "c", "zh", "zl", "y")
PLANE = ("x", "c", "y")
COLUMN = ("zh", "zl")
SWAP = [(0, 1), (1, 0)]
bf16 = jnp.bfloat16
f32 = jnp.float32


def answer_kernel(groups, slots, tb, banks, row_chunk, tags_ref, *refs):
    x_hbm, (w_hbm, bank_hbm), out_hbm = refs[:groups], refs[groups : groups + 2], refs[groups + 2 : 2 * groups + 2]
    (x_ref, w_ref, bank_ref, unit_ref, order_ref, count_ref, tile_bank, tile_first, tile_last, x_sem, w_sem, bank_sem, out_sem) = refs[2 * groups + 2 :]
    rows = slots * tb
    w_copy = pltpu.make_async_copy(w_hbm, w_ref, w_sem)
    bank_copy = pltpu.make_async_copy(bank_hbm, bank_ref, bank_sem)
    x_copies = [
        pltpu.make_async_copy(x_hbm[g], x_ref.at[pl.ds(g * rows, rows), :], x_sem.at[g]) for g in range(groups)
    ]
    w_copy.start()
    for copy in x_copies:
        copy.start()
    bank_copy.start()
    total = groups * slots

    for b in range(banks):
        count_ref[b] = 0

    def count(s, carry):
        b = tags_ref[s]
        count_ref[b] = count_ref[b] + 1
        return carry

    lax.fori_loop(0, total, count, 0)

    def lay(b, carry):
        first, tiles = carry
        n = count_ref[b]
        last = first + n - 1

        def tile(i, carry):
            tile_bank[tiles + i] = b
            tile_first[tiles + i] = first + i * TILE_SLOTS
            tile_last[tiles + i] = last
            return carry

        n_tiles = lax.div(n + TILE_SLOTS - 1, TILE_SLOTS)
        lax.fori_loop(0, n_tiles, tile, 0)
        count_ref[b] = first
        return first + n, tiles + n_tiles

    _, n_tiles = lax.fori_loop(0, banks, lay, (0, 0))

    def place(s, carry):
        b = tags_ref[s]
        at = count_ref[b]
        order_ref[at] = s
        count_ref[b] = at + 1
        return carry

    lax.fori_loop(0, total, place, 0)

    def project(i, carry):
        part = pl.ds(pl.multiple_of(i * row_chunk, row_chunk), row_chunk)
        projected = jnp.dot(x_ref[part, :], w_ref[...], preferred_element_type=f32)
        radius = jnp.sqrt(jnp.sum(projected * projected, axis=-1, keepdims=True) + norm_eps)
        unit_ref[part, :] = (projected * (1.0 / radius)).astype(bf16)
        return carry

    w_copy.wait()
    for copy in x_copies:
        copy.wait()
    lax.fori_loop(0, groups * rows // row_chunk, project, 0)
    bank_copy.wait()

    def answer_tile(t, carry):
        b = tile_bank[t]
        first = tile_first[t]
        last = tile_last[t]
        at = []
        for i in range(TILE_SLOTS):
            at.append(pl.multiple_of(order_ref[jnp.minimum(first + i, last)] * tb, tb))
        queries = jnp.concatenate([unit_ref[pl.ds(a, tb), :] for a in at], axis=0)
        keys = bank_ref[pl.ds(pl.multiple_of(b * BROWS, BROWS), BROWS), :]
        scores = lax.dot_general(queries, keys, (((1,), (1,)), ((), ())), preferred_element_type=f32)
        coef = jax.nn.sigmoid(logit_scale * scores + logit_bias).astype(bf16)
        grad = logit_scale * jnp.dot(coef, keys, preferred_element_type=f32)
        grad = grad.astype(bf16)
        for i, a in enumerate(at):
            x_ref[pl.ds(a, tb), :] = grad[i * tb : (i + 1) * tb, :]
        return carry

    lax.fori_loop(0, n_tiles, answer_tile, 0)
    out_copies = [
        pltpu.make_async_copy(x_ref.at[pl.ds(g * rows, rows), :], out_hbm[g], out_sem.at[g]) for g in range(groups)
    ]
    for copy in out_copies:
        copy.start()
    for copy in out_copies:
        copy.wait()


def answer(xs, tags, weight_half, bank, tb):
    groups = len(xs)
    rows, width = xs[0].shape
    slots = rows // tb
    banks = bank.shape[0] // BROWS
    most_tiles = groups * slots // TILE_SLOTS + banks + 1
    row_chunk = 128 if rows % 128 == 0 else tb
    hbm = pl.BlockSpec(memory_space=pltpu.HBM)
    return pl.pallas_call(
        functools.partial(answer_kernel, groups, slots, tb, banks, row_chunk),
        out_shape=[jax.ShapeDtypeStruct((rows, width), bf16)] * groups,
        in_specs=[pl.BlockSpec(memory_space=pltpu.SMEM)] + [hbm] * (groups + 2),
        out_specs=[hbm] * groups,
        scratch_shapes=[
            pltpu.VMEM((groups * rows, width), bf16),
            pltpu.VMEM(weight_half.shape, bf16),
            pltpu.VMEM(bank.shape, bf16),
            pltpu.VMEM((groups * rows, width), bf16),
            pltpu.SMEM((groups * slots,), jnp.int32),
            pltpu.SMEM((banks,), jnp.int32),
            pltpu.SMEM((most_tiles,), jnp.int32),
            pltpu.SMEM((most_tiles,), jnp.int32),
            pltpu.SMEM((most_tiles,), jnp.int32),
            pltpu.SemaphoreType.DMA((groups,)),
            pltpu.SemaphoreType.DMA,
            pltpu.SemaphoreType.DMA,
            pltpu.SemaphoreType.DMA((groups,)),
        ],
        compiler_params=pltpu.CompilerParams(vmem_limit_bytes=60 << 20),
        cost_estimate=pl.CostEstimate(
            flops=groups * (2 * rows * width * width + 8 * rows * width * BROWS),
            bytes_accessed=groups * 4 * rows * width + 2 * width * width + 2 * bank.size,
            transcendentals=groups * rows * BROWS,
        ),
        name="answer",
    )(tags, *xs, weight_half, bank)


def finish_kernel(n_x, n_z, n_y, piece, c_ref, base_ref, high_ref, unit_ref, radius_ref, text_ref, p_ref, send_ref, keep_ref, g_ref):
    at = pl.program_id(0)
    embed = base_ref[...] + high_ref[...].astype(f32)
    unit = unit_ref[...]
    radial = jnp.sum(unit * embed, axis=-1, keepdims=True)
    p = ((embed - unit * radial) / radius_ref[...]).astype(bf16)
    p_ref[...] = p
    grad = jnp.dot(text_ref[...], p, preferred_element_type=f32)

    @pl.when(at == 0)
    def _():
        g_ref[...] = grad

    @pl.when(at > 0)
    def _():
        g_ref[...] += grad

    for core in range(2):

        @pl.when((at == pl.num_programs(0) - 1) & (c_ref[0] == core))
        def _():
            for x in range(n_x):
                for y in range(n_y):
                    for z in range(n_z):
                        mine = (((x * 2 + core) * n_z + z) * n_y + y) * piece
                        other = (((x * 2 + 1 - core) * n_z + z) * n_y + y) * piece
                        keep_ref[x * n_y + y, z, :piece, :] = g_ref[mine : mine + piece, :]
                        send_ref[x * n_y + y, z, :piece, :] = g_ref[other : other + piece, :].astype(bf16)


def finish(c, base, from_high, unit_rows, radius, text_t, n_x, n_z, n_y):
    rows, width = base.shape
    depth = text_t.shape[0]
    piece = depth // (n_x * 2 * n_z * n_y)
    tall = piece + -piece % 8
    steps = 2
    block = rows // steps
    by_row = pl.BlockSpec((block, width), lambda i: (i, 0))
    whole = pl.BlockSpec((n_x * n_y, n_z, tall, width), lambda i: (0, 0, 0, 0))
    return pl.pallas_call(
        functools.partial(finish_kernel, n_x, n_z, n_y, piece),
        grid=(steps,),
        out_shape=[
            jax.ShapeDtypeStruct((rows, width), bf16),
            jax.ShapeDtypeStruct((n_x * n_y, n_z, tall, width), bf16),
            jax.ShapeDtypeStruct((n_x * n_y, n_z, tall, width), f32),
        ],
        in_specs=[
            pl.BlockSpec(memory_space=pltpu.SMEM),
            by_row,
            by_row,
            by_row,
            pl.BlockSpec((block, 1), lambda i: (i, 0)),
            pl.BlockSpec((depth, block), lambda i: (0, i)),
        ],
        out_specs=[by_row, whole, whole],
        scratch_shapes=[pltpu.VMEM((depth, width), f32)],
        compiler_params=pltpu.CompilerParams(vmem_limit_bytes=40 << 20),
        cost_estimate=pl.CostEstimate(
            flops=2 * rows * depth * width, bytes_accessed=16 * rows * width + 6 * depth * width, transcendentals=rows
        ),
        name="finish",
    )(c.reshape(1), base, from_high, unit_rows, radius, text_t)


def slots_of(named, values, capacity):
    visits = named.shape[-1]
    order = jnp.arange(visits, dtype=jnp.int32)
    before = (order[:, None] < order[None, :]).astype(bf16)
    rank = jnp.dot(named.astype(bf16), before, preferred_element_type=f32)
    hit = named[..., None, :] & (rank[..., None, :] == jnp.arange(capacity, dtype=f32)[:, None])
    return jnp.sum(jnp.where(hit, values[..., None, :] + 1, 0), axis=-1) - 1


def route(owners, blocks, capacity):
    n_blocks, hard = owners.shape
    visits = n_blocks * hard
    n_x, n_c, n_h, n_l, n_y = (lax.axis_size(a) for a in ALL)
    x, c, zh, zl, y = (lax.axis_index(a) for a in ALL)
    n_z, devices = n_h * n_l, n_x * n_c * n_h * n_l * n_y
    xs, cs, ys = jnp.arange(n_x), jnp.arange(n_c), jnp.arange(n_y)
    z_at = zh * n_l + zl
    dest = (((xs[:, None, None] * n_c + cs[None, :, None]) * n_z) + z_at) * n_y + ys[None, None, :]
    dest = dest.reshape(-1, 1)
    me = ((x * n_c + c) * n_z + z_at) * n_y + y
    text_block = jnp.arange(visits, dtype=jnp.int32) // hard
    mine = owners.reshape(1, visits)
    first = slots_of(mine == dest, text_block[None], capacity).reshape(-1)

    pad = -(2 * visits) % 1024
    own = jnp.concatenate([owners.reshape(-1), blocks.reshape(-1), jnp.zeros((pad,), jnp.int32)])
    table = jnp.broadcast_to(own.reshape(1, -1, 128), (devices, own.shape[0] // 128, 128))
    table = lax.all_to_all(table, ALL, split_axis=0, concat_axis=0, tiled=True)
    table = table.reshape(n_x, n_c, n_h, n_l, n_y, -1)
    table = jnp.where(zh == 0, table, jnp.flip(table, 2))
    table = jnp.where(zl == 0, table, jnp.flip(table, 3))
    table = table.transpose(2, 3, 0, 1, 4, 5).reshape(n_z, n_x * n_c * n_y, -1)
    plane_at = (x * n_c + c) * n_y + y
    column = lax.dynamic_index_in_dim(table, plane_at, 1, keepdims=False)[1:, None, :visits]
    others = slots_of(column == dest, text_block, capacity).reshape(n_z - 1, -1)
    tags = slots_of(table[:, :, :visits] == me, table[:, :, visits : 2 * visits], capacity).reshape(n_z, -1)
    return [first] + [others[k] for k in range(n_z - 1)], jnp.maximum(tags, 0)


def gather_weight(proj):
    n_x, n_c, n_h, n_l, n_y = (lax.axis_size(a) for a in ALL)
    x, c, zh, zl, y = (lax.axis_index(a) for a in ALL)
    rows, width = proj.shape
    n_z, n_xy = n_h * n_l, n_x * n_y
    piece = jnp.pad(proj.astype(bf16), ((0, -rows % 8), (0, 0)))[None]
    column = [piece]
    for k in range(1, n_z):
        column.append(lax.ppermute(piece, COLUMN, [(i, i ^ k) for i in range(n_z)]))
    piece = jnp.concatenate(column)
    flat = [piece]
    for k in range(1, n_xy):
        flat.append(lax.ppermute(piece, ("x", "y"), [(i, i ^ k) for i in range(n_xy)]))
    piece = jnp.concatenate(flat)
    other = lax.ppermute(piece, "c", SWAP)
    piece = jnp.concatenate([piece, other])
    xs, cs, zs, ys = jnp.arange(n_x), jnp.arange(n_c), jnp.arange(n_z), jnp.arange(n_y)
    far_c = (cs ^ c)[None, :, None, None]
    far_xy = ((xs[:, None] * n_y + ys[None, :]) ^ (x * n_y + y))[:, None, None, :]
    far_z = (zs ^ (zh * n_l + zl))[None, None, :, None]
    at = ((far_c * n_xy + far_xy) * n_z + far_z).reshape(-1)
    return jnp.take(piece, at, axis=0)[:, :rows].reshape(-1, width)


def reduce_weight(send, keep, rows):
    n_xy, n_z, tall, width = send.shape
    other = lax.ppermute(send, "c", SWAP)
    total = (keep + other.astype(f32)).astype(bf16).reshape(n_xy, n_z * tall, width)
    total = lax.all_to_all(total, ("x", "y"), split_axis=0, concat_axis=0, tiled=True)
    total = jnp.sum(total.astype(f32), axis=0).reshape(n_z, tall, width).astype(bf16)
    total = lax.all_to_all(total, COLUMN, split_axis=0, concat_axis=0, tiled=True)
    return jnp.sum(total.astype(f32), axis=0)[:rows]


def step(text_feats, proj, first_moment, second_moment, owners, blocks, positives, bank):
    devices = lax.axis_size(ALL)
    plane = lax.axis_size(PLANE)
    rows_dev, _ = text_feats.shape
    text_blocks, hard = owners.shape
    tb = rows_dev // text_blocks
    visits = text_blocks * hard
    capacity = max(2, visits // devices + 1)

    text_high = lax.ppermute(text_feats, "zh", SWAP)
    text_low = lax.ppermute(text_feats, "zl", SWAP)
    text_far = lax.ppermute(text_high, "zl", SWAP)
    sources, tags = route(owners, blocks, capacity)
    text_far, weight_half, tags = lax.optimization_barrier((text_far, gather_weight(proj), tags))
    texts = (text_feats, text_low, text_high, text_far)

    def exchange(rows):
        rows = rows.reshape(plane, capacity * tb, -1)
        rows = lax.all_to_all(rows, PLANE, split_axis=0, concat_axis=0, tiled=True)
        return rows.reshape(plane * capacity * tb, -1)

    picks, got, replies, partial = [], [], [], []
    for k in range(4):
        row_of = sources[k][:, None] * tb + jnp.arange(tb, dtype=jnp.int32)[None, :]
        row_of = jnp.where(sources[k][:, None] >= 0, row_of, -1).reshape(-1)
        pick = (row_of[:, None] == jnp.arange(rows_dev, dtype=jnp.int32)[None, :]).astype(bf16)
        sent = jnp.dot(pick, texts[k], preferred_element_type=f32).astype(bf16)
        picks.append(pick)
        got.append(exchange(sent))
    replies += answer(got[:3], tags[:3].reshape(-1), weight_half, bank, tb)
    replies += answer(got[3:], tags[3], weight_half, bank, tb)
    for k in range(4):
        reply = exchange(replies[k])
        partial.append(
            lax.dot_general(picks[k], reply, (((0,), (0,)), ((), ())), preferred_element_type=f32)
        )
    from_far = lax.ppermute(partial[3].astype(bf16), "zl", SWAP)
    from_high = lax.ppermute((partial[2] + from_far.astype(f32)).astype(bf16), "zh", SWAP)
    from_low = lax.ppermute(partial[1].astype(bf16), "zl", SWAP)
    projected = jnp.dot(text_feats, weight_half, preferred_element_type=f32)
    radius = jnp.sqrt(jnp.sum(projected * projected, axis=-1, keepdims=True) + norm_eps)
    unit_rows = projected / radius
    unit_half = unit_rows.astype(bf16)
    scores = logit_scale * jnp.dot(unit_half, bank.T, preferred_element_type=f32) + logit_bias
    columns = jnp.arange(bank.shape[0], dtype=jnp.int32)
    labels = jnp.where(columns[None, :] == positives[:, None], 1.0, -1.0).astype(f32)
    local_coef = (-labels * jax.nn.sigmoid(-labels * scores)).astype(bf16)
    local_grad = logit_scale * jnp.dot(local_coef, bank, preferred_element_type=f32)
    local_grad, unit_rows, radius = lax.optimization_barrier((local_grad, unit_rows, radius))

    base = local_grad + partial[0] + from_low.astype(f32)
    n_x, n_z, n_y = lax.axis_size("x"), lax.axis_size(COLUMN), lax.axis_size("y")
    proj_grad_rows, send, keep = finish(
        lax.axis_index("c").astype(jnp.int32), base, from_high, unit_rows, radius, text_feats.T, n_x, n_z, n_y
    )
    weight_grad = reduce_weight(send, keep, proj.shape[0])
    text_grad = lax.dot_general(
        proj_grad_rows, weight_half, (((1,), (1,)), ((), ())), preferred_element_type=f32
    ).astype(bf16)
    new_first = beta_one * first_moment + (1.0 - beta_one) * weight_grad
    new_second = beta_two * second_moment + (1.0 - beta_two) * weight_grad * weight_grad
    first_hat = new_first / (1.0 - beta_one**adam_step)
    second_hat = new_second / (1.0 - beta_two**adam_step)
    new_proj = proj - learn_rate * (first_hat / (jnp.sqrt(second_hat) + adam_eps) + decay_rate * proj)
    return (text_grad, new_proj, new_first, new_second)


def solution(mesh):
    n_gx, n_gy = mesh.shape["gx"], mesh.shape["gy"]
    fine = Mesh(mesh.devices.reshape(n_gx // 2, 2, 2, 2, n_gy // 4), ALL)
    rows = P(ALL, None)
    return jax.shard_map(
        step,
        mesh=fine,
        in_specs=(rows, rows, rows, rows, rows, rows, P(ALL), rows),
        out_specs=(rows, rows, rows, rows),
        check_vma=False,
    )
```

```python
import functools

import jax
import jax.numpy as jnp
from jax import lax
from jax.experimental import pallas as pl
from jax.experimental.pallas import tpu as pltpu
from jax.sharding import Mesh, PartitionSpec as P


BROWS = 256
TILE_SLOTS = 8

logit_scale = 20.0
logit_bias = -3.0
norm_eps = 1e-06
beta_one = 0.9
beta_two = 0.999
learn_rate = 0.001
decay_rate = 0.1
adam_eps = 1e-08
adam_step = 100.0

ALL = ("x", "c", "zh", "zl", "y")
PLANE = ("x", "c", "y")
COLUMN = ("zh", "zl")
SWAP = [(0, 1), (1, 0)]
bf16 = jnp.bfloat16
f32 = jnp.float32


def answer_kernel(groups, slots, tb, banks, row_chunk, tags_ref, *refs):
    x_hbm, (w_hbm, bank_hbm), out_hbm = refs[:groups], refs[groups : groups + 2], refs[groups + 2 : 2 * groups + 2]
    (x_ref, w_ref, bank_ref, unit_ref, order_ref, count_ref, tile_bank, tile_first, tile_last, x_sem, w_sem, bank_sem, out_sem) = refs[2 * groups + 2 :]
    rows = slots * tb
    w_copy = pltpu.make_async_copy(w_hbm, w_ref, w_sem)
    bank_copy = pltpu.make_async_copy(bank_hbm, bank_ref, bank_sem)
    x_copies = [
        pltpu.make_async_copy(x_hbm[g], x_ref.at[pl.ds(g * rows, rows), :], x_sem.at[g]) for g in range(groups)
    ]
    w_copy.start()
    for copy in x_copies:
        copy.start()
    bank_copy.start()
    total = groups * slots

    for b in range(banks):
        count_ref[b] = 0

    def count(s, carry):
        b = tags_ref[s]
        count_ref[b] = count_ref[b] + 1
        return carry

    lax.fori_loop(0, total, count, 0)

    def lay(b, carry):
        first, tiles = carry
        n = count_ref[b]
        last = first + n - 1

        def tile(i, carry):
            tile_bank[tiles + i] = b
            tile_first[tiles + i] = first + i * TILE_SLOTS
            tile_last[tiles + i] = last
            return carry

        n_tiles = lax.div(n + TILE_SLOTS - 1, TILE_SLOTS)
        lax.fori_loop(0, n_tiles, tile, 0)
        count_ref[b] = first
        return first + n, tiles + n_tiles

    _, n_tiles = lax.fori_loop(0, banks, lay, (0, 0))

    def place(s, carry):
        b = tags_ref[s]
        at = count_ref[b]
        order_ref[at] = s
        count_ref[b] = at + 1
        return carry

    lax.fori_loop(0, total, place, 0)

    def project(i, carry):
        part = pl.ds(pl.multiple_of(i * row_chunk, row_chunk), row_chunk)
        projected = jnp.dot(x_ref[part, :], w_ref[...], preferred_element_type=f32)
        radius = jnp.sqrt(jnp.sum(projected * projected, axis=-1, keepdims=True) + norm_eps)
        unit_ref[part, :] = (projected * (1.0 / radius)).astype(bf16)
        return carry

    w_copy.wait()
    for copy in x_copies:
        copy.wait()
    lax.fori_loop(0, groups * rows // row_chunk, project, 0)
    bank_copy.wait()

    def answer_tile(t, carry):
        b = tile_bank[t]
        first = tile_first[t]
        last = tile_last[t]
        at = []
        for i in range(TILE_SLOTS):
            at.append(pl.multiple_of(order_ref[jnp.minimum(first + i, last)] * tb, tb))
        queries = jnp.concatenate([unit_ref[pl.ds(a, tb), :] for a in at], axis=0)
        keys = bank_ref[pl.ds(pl.multiple_of(b * BROWS, BROWS), BROWS), :]
        scores = lax.dot_general(queries, keys, (((1,), (1,)), ((), ())), preferred_element_type=f32)
        coef = jax.nn.sigmoid(logit_scale * scores + logit_bias).astype(bf16)
        grad = logit_scale * jnp.dot(coef, keys, preferred_element_type=f32)
        grad = grad.astype(bf16)
        for i, a in enumerate(at):
            x_ref[pl.ds(a, tb), :] = grad[i * tb : (i + 1) * tb, :]
        return carry

    lax.fori_loop(0, n_tiles, answer_tile, 0)
    out_copies = [
        pltpu.make_async_copy(x_ref.at[pl.ds(g * rows, rows), :], out_hbm[g], out_sem.at[g]) for g in range(groups)
    ]
    for copy in out_copies:
        copy.start()
    for copy in out_copies:
        copy.wait()


def answer(xs, tags, weight_half, bank, tb):
    groups = len(xs)
    rows, width = xs[0].shape
    slots = rows // tb
    banks = bank.shape[0] // BROWS
    most_tiles = groups * slots // TILE_SLOTS + banks + 1
    row_chunk = 128 if rows % 128 == 0 else tb
    hbm = pl.BlockSpec(memory_space=pltpu.HBM)
    return pl.pallas_call(
        functools.partial(answer_kernel, groups, slots, tb, banks, row_chunk),
        out_shape=[jax.ShapeDtypeStruct((rows, width), bf16)] * groups,
        in_specs=[pl.BlockSpec(memory_space=pltpu.SMEM)] + [hbm] * (groups + 2),
        out_specs=[hbm] * groups,
        scratch_shapes=[
            pltpu.VMEM((groups * rows, width), bf16),
            pltpu.VMEM(weight_half.shape, bf16),
            pltpu.VMEM(bank.shape, bf16),
            pltpu.VMEM((groups * rows, width), bf16),
            pltpu.SMEM((groups * slots,), jnp.int32),
            pltpu.SMEM((banks,), jnp.int32),
            pltpu.SMEM((most_tiles,), jnp.int32),
            pltpu.SMEM((most_tiles,), jnp.int32),
            pltpu.SMEM((most_tiles,), jnp.int32),
            pltpu.SemaphoreType.DMA((groups,)),
            pltpu.SemaphoreType.DMA,
            pltpu.SemaphoreType.DMA,
            pltpu.SemaphoreType.DMA((groups,)),
        ],
        compiler_params=pltpu.CompilerParams(vmem_limit_bytes=60 << 20),
        cost_estimate=pl.CostEstimate(
            flops=groups * (2 * rows * width * width + 8 * rows * width * BROWS),
            bytes_accessed=groups * 4 * rows * width + 2 * width * width + 2 * bank.size,
            transcendentals=groups * rows * BROWS,
        ),
        name="answer",
    )(tags, *xs, weight_half, bank)


def finish_kernel(n_x, n_z, n_y, piece, c_ref, base_ref, high_ref, unit_ref, radius_ref, text_ref, p_ref, send_ref, keep_ref, g_ref):
    at = pl.program_id(0)
    embed = base_ref[...] + high_ref[...].astype(f32)
    unit = unit_ref[...]
    radial = jnp.sum(unit * embed, axis=-1, keepdims=True)
    p = ((embed - unit * radial) / radius_ref[...]).astype(bf16)
    p_ref[...] = p
    grad = jnp.dot(text_ref[...], p, preferred_element_type=f32)

    @pl.when(at == 0)
    def _():
        g_ref[...] = grad

    @pl.when(at > 0)
    def _():
        g_ref[...] += grad

    for core in range(2):

        @pl.when((at == pl.num_programs(0) - 1) & (c_ref[0] == core))
        def _():
            for x in range(n_x):
                for y in range(n_y):
                    for z in range(n_z):
                        mine = (((x * 2 + core) * n_z + z) * n_y + y) * piece
                        other = (((x * 2 + 1 - core) * n_z + z) * n_y + y) * piece
                        keep_ref[x * n_y + y, z, :piece, :] = g_ref[mine : mine + piece, :]
                        send_ref[x * n_y + y, z, :piece, :] = g_ref[other : other + piece, :].astype(bf16)


def finish(c, base, from_high, unit_rows, radius, text_t, n_x, n_z, n_y):
    rows, width = base.shape
    depth = text_t.shape[0]
    piece = depth // (n_x * 2 * n_z * n_y)
    tall = piece + -piece % 8
    steps = 2
    block = rows // steps
    by_row = pl.BlockSpec((block, width), lambda i: (i, 0))
    whole = pl.BlockSpec((n_x * n_y, n_z, tall, width), lambda i: (0, 0, 0, 0))
    return pl.pallas_call(
        functools.partial(finish_kernel, n_x, n_z, n_y, piece),
        grid=(steps,),
        out_shape=[
            jax.ShapeDtypeStruct((rows, width), bf16),
            jax.ShapeDtypeStruct((n_x * n_y, n_z, tall, width), bf16),
            jax.ShapeDtypeStruct((n_x * n_y, n_z, tall, width), f32),
        ],
        in_specs=[
            pl.BlockSpec(memory_space=pltpu.SMEM),
            by_row,
            by_row,
            by_row,
            pl.BlockSpec((block, 1), lambda i: (i, 0)),
            pl.BlockSpec((depth, block), lambda i: (0, i)),
        ],
        out_specs=[by_row, whole, whole],
        scratch_shapes=[pltpu.VMEM((depth, width), f32)],
        compiler_params=pltpu.CompilerParams(vmem_limit_bytes=40 << 20),
        cost_estimate=pl.CostEstimate(
            flops=2 * rows * depth * width, bytes_accessed=16 * rows * width + 6 * depth * width, transcendentals=rows
        ),
        name="finish",
    )(c.reshape(1), base, from_high, unit_rows, radius, text_t)


def slots_of(named, values, capacity):
    visits = named.shape[-1]
    order = jnp.arange(visits, dtype=jnp.int32)
    before = (order[:, None] < order[None, :]).astype(bf16)
    rank = jnp.dot(named.astype(bf16), before, preferred_element_type=f32)
    hit = named[..., None, :] & (rank[..., None, :] == jnp.arange(capacity, dtype=f32)[:, None])
    return jnp.sum(jnp.where(hit, values[..., None, :] + 1, 0), axis=-1) - 1


def gather_weight(proj, owners, blocks):
    n_x, n_c, n_h, n_l, n_y = (lax.axis_size(a) for a in ALL)
    x, c, zh, zl, y = (lax.axis_index(a) for a in ALL)
    rows, width = proj.shape
    n_z, n_xy = n_h * n_l, n_x * n_y
    listed = jnp.concatenate([owners.reshape(-1), blocks.reshape(-1)]).astype(bf16)
    entries = listed.shape[0]
    list_rows = -(-entries // width)
    listed = jnp.pad(listed, (0, list_rows * width - entries)).reshape(list_rows, width)
    piece = jnp.concatenate([proj.astype(bf16), listed])
    piece = jnp.pad(piece, ((0, -(rows + list_rows) % 8), (0, 0)))[None]
    column = [piece]
    for k in range(1, n_z):
        column.append(lax.ppermute(piece, COLUMN, [(i, i ^ k) for i in range(n_z)]))
    piece = jnp.concatenate(column)
    column_lists = piece[:, rows : rows + list_rows].reshape(n_z, -1)[:, :entries].astype(jnp.int32)
    flat = [piece]
    for k in range(1, n_xy):
        flat.append(lax.ppermute(piece, ("x", "y"), [(i, i ^ k) for i in range(n_xy)]))
    piece = jnp.concatenate(flat)
    other = lax.ppermute(piece, "c", SWAP)
    piece = jnp.concatenate([piece, other])
    xs, cs, zs, ys = jnp.arange(n_x), jnp.arange(n_c), jnp.arange(n_z), jnp.arange(n_y)
    far_c = (cs ^ c)[None, :, None, None]
    far_xy = ((xs[:, None] * n_y + ys[None, :]) ^ (x * n_y + y))[:, None, None, :]
    far_z = (zs ^ (zh * n_l + zl))[None, None, :, None]
    at = ((far_c * n_xy + far_xy) * n_z + far_z).reshape(-1)
    piece = jnp.take(piece, at, axis=0)
    lists = piece[:, rows : rows + list_rows].reshape(piece.shape[0], -1)[:, :entries].astype(jnp.int32)
    return piece[:, :rows].reshape(-1, width), column_lists, lists


def route(owners, column_lists, lists, capacity):
    n_blocks, hard = owners.shape
    visits = n_blocks * hard
    n_x, n_c, n_h, n_l, n_y = (lax.axis_size(a) for a in ALL)
    x, c, zh, zl, y = (lax.axis_index(a) for a in ALL)
    n_z = n_h * n_l
    xs, cs, ys = jnp.arange(n_x), jnp.arange(n_c), jnp.arange(n_y)
    z_at = zh * n_l + zl
    dest = (((xs[:, None, None] * n_c + cs[None, :, None]) * n_z) + z_at) * n_y + ys[None, None, :]
    dest = dest.reshape(-1, 1)
    me = ((x * n_c + c) * n_z + z_at) * n_y + y
    text_block = jnp.arange(visits, dtype=jnp.int32) // hard
    first = slots_of(owners.reshape(1, visits) == dest, text_block[None], capacity).reshape(-1)
    others = slots_of(column_lists[1:, None, :visits] == dest, text_block, capacity).reshape(n_z - 1, -1)
    table = lists.reshape(n_x, n_c, n_h, n_l, n_y, -1)
    table = jnp.where(zh == 0, table, jnp.flip(table, 2))
    table = jnp.where(zl == 0, table, jnp.flip(table, 3))
    table = table.transpose(2, 3, 0, 1, 4, 5).reshape(n_z, n_x * n_c * n_y, -1)
    tags = slots_of(table[:, :, :visits] == me, table[:, :, visits:], capacity).reshape(n_z, -1)
    return [first] + [others[k] for k in range(n_z - 1)], jnp.maximum(tags, 0)


def reduce_weight(send, keep, rows):
    n_xy, n_z, tall, width = send.shape
    other = lax.ppermute(send, "c", SWAP)
    total = (keep + other.astype(f32)).astype(bf16).reshape(n_xy, n_z * tall, width)
    total = lax.all_to_all(total, ("x", "y"), split_axis=0, concat_axis=0, tiled=True)
    total = jnp.sum(total.astype(f32), axis=0).reshape(n_z, tall, width).astype(bf16)
    total = lax.all_to_all(total, COLUMN, split_axis=0, concat_axis=0, tiled=True)
    return jnp.sum(total.astype(f32), axis=0)[:rows]


def step(text_feats, proj, first_moment, second_moment, owners, blocks, positives, bank):
    devices = lax.axis_size(ALL)
    plane = lax.axis_size(PLANE)
    rows_dev, _ = text_feats.shape
    text_blocks, hard = owners.shape
    tb = rows_dev // text_blocks
    visits = text_blocks * hard
    capacity = max(2, visits // devices + 1)

    text_low = lax.ppermute(text_feats, "zl", SWAP)
    text_high = lax.ppermute(text_feats, "zh", SWAP)
    text_far = lax.ppermute(text_high, "zl", SWAP)
    weight_half, column_lists, lists = gather_weight(proj, owners, blocks)
    sources, tags = route(owners, column_lists, lists, capacity)
    texts = (text_feats, text_low, text_high, text_far)

    def exchange(rows):
        rows = rows.reshape(plane, capacity * tb, -1)
        rows = lax.all_to_all(rows, PLANE, split_axis=0, concat_axis=0, tiled=True)
        return rows.reshape(plane * capacity * tb, -1)

    picks, got, replies, partial = [], [], [], []
    for k in range(4):
        row_of = sources[k][:, None] * tb + jnp.arange(tb, dtype=jnp.int32)[None, :]
        row_of = jnp.where(sources[k][:, None] >= 0, row_of, -1).reshape(-1)
        pick = (row_of[:, None] == jnp.arange(rows_dev, dtype=jnp.int32)[None, :]).astype(bf16)
        sent = jnp.dot(pick, texts[k], preferred_element_type=f32).astype(bf16)
        picks.append(pick)
        got.append(exchange(sent))
    replies += answer(got[:2], tags[:2].reshape(-1), weight_half, bank, tb)
    replies += answer(got[2:3], tags[2], weight_half, bank, tb)
    replies += answer(got[3:], tags[3], weight_half, bank, tb)
    for k in range(4):
        reply = exchange(replies[k])
        partial.append(
            lax.dot_general(picks[k], reply, (((0,), (0,)), ((), ())), preferred_element_type=f32)
        )
    from_far = lax.ppermute(partial[3].astype(bf16), "zl", SWAP)
    from_high = lax.ppermute((partial[2] + from_far.astype(f32)).astype(bf16), "zh", SWAP)
    from_low = lax.ppermute(partial[1].astype(bf16), "zl", SWAP)
    projected = jnp.dot(text_feats, weight_half, preferred_element_type=f32)
    radius = jnp.sqrt(jnp.sum(projected * projected, axis=-1, keepdims=True) + norm_eps)
    unit_rows = projected / radius
    unit_half = unit_rows.astype(bf16)
    scores = logit_scale * jnp.dot(unit_half, bank.T, preferred_element_type=f32) + logit_bias
    columns = jnp.arange(bank.shape[0], dtype=jnp.int32)
    labels = jnp.where(columns[None, :] == positives[:, None], 1.0, -1.0).astype(f32)
    local_coef = (-labels * jax.nn.sigmoid(-labels * scores)).astype(bf16)
    local_grad = logit_scale * jnp.dot(local_coef, bank, preferred_element_type=f32)
    local_grad, unit_rows, radius = lax.optimization_barrier((local_grad, unit_rows, radius))

    base = local_grad + partial[0] + from_low.astype(f32)
    n_x, n_z, n_y = lax.axis_size("x"), lax.axis_size(COLUMN), lax.axis_size("y")
    proj_grad_rows, send, keep = finish(
        lax.axis_index("c").astype(jnp.int32), base, from_high, unit_rows, radius, text_feats.T, n_x, n_z, n_y
    )
    weight_grad = reduce_weight(send, keep, proj.shape[0])
    text_grad = lax.dot_general(
        proj_grad_rows, weight_half, (((1,), (1,)), ((), ())), preferred_element_type=f32
    ).astype(bf16)
    new_first = beta_one * first_moment + (1.0 - beta_one) * weight_grad
    new_second = beta_two * second_moment + (1.0 - beta_two) * weight_grad * weight_grad
    first_hat = new_first / (1.0 - beta_one**adam_step)
    second_hat = new_second / (1.0 - beta_two**adam_step)
    new_proj = proj - learn_rate * (first_hat / (jnp.sqrt(second_hat) + adam_eps) + decay_rate * proj)
    return (text_grad, new_proj, new_first, new_second)


def solution(mesh):
    n_gx, n_gy = mesh.shape["gx"], mesh.shape["gy"]
    fine = Mesh(mesh.devices.reshape(n_gx // 2, 2, 2, 2, n_gy // 4), ALL)
    rows = P(ALL, None)
    return jax.shard_map(
        step,
        mesh=fine,
        in_specs=(rows, rows, rows, rows, rows, rows, P(ALL), rows),
        out_specs=(rows, rows, rows, rows),
        check_vma=False,
    )
```

```python
import functools

import jax
import jax.numpy as jnp
from jax import lax
from jax.experimental import pallas as pl
from jax.experimental.pallas import tpu as pltpu
from jax.sharding import Mesh, PartitionSpec as P


BROWS = 256
TILE_SLOTS = 8

logit_scale = 20.0
logit_bias = -3.0
norm_eps = 1e-06
beta_one = 0.9
beta_two = 0.999
learn_rate = 0.001
decay_rate = 0.1
adam_eps = 1e-08
adam_step = 100.0

ALL = ("x", "c", "zh", "zl", "y")
PLANE = ("x", "c", "y")
COLUMN = ("zh", "zl")
SWAP = [(0, 1), (1, 0)]
bf16 = jnp.bfloat16
f32 = jnp.float32


def answer_kernel(groups, slots, tb, banks, row_chunk, tags_ref, *refs):
    x_hbm, (w_hbm, bank_hbm), out_hbm = refs[:groups], refs[groups : groups + 2], refs[groups + 2 : 2 * groups + 2]
    (x_ref, w_ref, bank_ref, unit_ref, order_ref, count_ref, tile_bank, tile_first, tile_last, x_sem, w_sem, bank_sem, out_sem) = refs[2 * groups + 2 :]
    rows = slots * tb
    w_copy = pltpu.make_async_copy(w_hbm, w_ref, w_sem)
    bank_copy = pltpu.make_async_copy(bank_hbm, bank_ref, bank_sem)
    x_copies = [
        pltpu.make_async_copy(x_hbm[g], x_ref.at[pl.ds(g * rows, rows), :], x_sem.at[g]) for g in range(groups)
    ]
    w_copy.start()
    for copy in x_copies:
        copy.start()
    bank_copy.start()
    total = groups * slots

    for b in range(banks):
        count_ref[b] = 0

    def count(s, carry):
        b = tags_ref[s]
        count_ref[b] = count_ref[b] + 1
        return carry

    lax.fori_loop(0, total, count, 0)

    def lay(b, carry):
        first, tiles = carry
        n = count_ref[b]
        last = first + n - 1

        def tile(i, carry):
            tile_bank[tiles + i] = b
            tile_first[tiles + i] = first + i * TILE_SLOTS
            tile_last[tiles + i] = last
            return carry

        n_tiles = lax.div(n + TILE_SLOTS - 1, TILE_SLOTS)
        lax.fori_loop(0, n_tiles, tile, 0)
        count_ref[b] = first
        return first + n, tiles + n_tiles

    _, n_tiles = lax.fori_loop(0, banks, lay, (0, 0))

    def place(s, carry):
        b = tags_ref[s]
        at = count_ref[b]
        order_ref[at] = s
        count_ref[b] = at + 1
        return carry

    lax.fori_loop(0, total, place, 0)

    def project(i, carry):
        part = pl.ds(pl.multiple_of(i * row_chunk, row_chunk), row_chunk)
        projected = jnp.dot(x_ref[part, :], w_ref[...], preferred_element_type=f32)
        radius = jnp.sqrt(jnp.sum(projected * projected, axis=-1, keepdims=True) + norm_eps)
        unit_ref[part, :] = (projected * (1.0 / radius)).astype(bf16)
        return carry

    w_copy.wait()
    for copy in x_copies:
        copy.wait()
    lax.fori_loop(0, groups * rows // row_chunk, project, 0)
    bank_copy.wait()

    def answer_tile(t, carry):
        b = tile_bank[t]
        first = tile_first[t]
        last = tile_last[t]
        at = []
        for i in range(TILE_SLOTS):
            at.append(pl.multiple_of(order_ref[jnp.minimum(first + i, last)] * tb, tb))
        queries = jnp.concatenate([unit_ref[pl.ds(a, tb), :] for a in at], axis=0)
        keys = bank_ref[pl.ds(pl.multiple_of(b * BROWS, BROWS), BROWS), :]
        scores = lax.dot_general(queries, keys, (((1,), (1,)), ((), ())), preferred_element_type=f32)
        coef = jax.nn.sigmoid(logit_scale * scores + logit_bias).astype(bf16)
        grad = logit_scale * jnp.dot(coef, keys, preferred_element_type=f32)
        grad = grad.astype(bf16)
        for i, a in enumerate(at):
            x_ref[pl.ds(a, tb), :] = grad[i * tb : (i + 1) * tb, :]
        return carry

    lax.fori_loop(0, n_tiles, answer_tile, 0)
    out_copies = [
        pltpu.make_async_copy(x_ref.at[pl.ds(g * rows, rows), :], out_hbm[g], out_sem.at[g]) for g in range(groups)
    ]
    for copy in out_copies:
        copy.start()
    for copy in out_copies:
        copy.wait()


def answer(xs, tags, weight_half, bank, tb):
    groups = len(xs)
    rows, width = xs[0].shape
    slots = rows // tb
    banks = bank.shape[0] // BROWS
    most_tiles = groups * slots // TILE_SLOTS + banks + 1
    row_chunk = 128 if rows % 128 == 0 else tb
    hbm = pl.BlockSpec(memory_space=pltpu.HBM)
    return pl.pallas_call(
        functools.partial(answer_kernel, groups, slots, tb, banks, row_chunk),
        out_shape=[jax.ShapeDtypeStruct((rows, width), bf16)] * groups,
        in_specs=[pl.BlockSpec(memory_space=pltpu.SMEM)] + [hbm] * (groups + 2),
        out_specs=[hbm] * groups,
        scratch_shapes=[
            pltpu.VMEM((groups * rows, width), bf16),
            pltpu.VMEM(weight_half.shape, bf16),
            pltpu.VMEM(bank.shape, bf16),
            pltpu.VMEM((groups * rows, width), bf16),
            pltpu.SMEM((groups * slots,), jnp.int32),
            pltpu.SMEM((banks,), jnp.int32),
            pltpu.SMEM((most_tiles,), jnp.int32),
            pltpu.SMEM((most_tiles,), jnp.int32),
            pltpu.SMEM((most_tiles,), jnp.int32),
            pltpu.SemaphoreType.DMA((groups,)),
            pltpu.SemaphoreType.DMA,
            pltpu.SemaphoreType.DMA,
            pltpu.SemaphoreType.DMA((groups,)),
        ],
        compiler_params=pltpu.CompilerParams(vmem_limit_bytes=60 << 20),
        cost_estimate=pl.CostEstimate(
            flops=groups * (2 * rows * width * width + 8 * rows * width * BROWS),
            bytes_accessed=groups * 4 * rows * width + 2 * width * width + 2 * bank.size,
            transcendentals=groups * rows * BROWS,
        ),
        name="answer",
    )(tags, *xs, weight_half, bank)


def finish_kernel(n_x, n_z, n_y, piece, c_ref, base_ref, high_ref, unit_ref, radius_ref, text_ref, p_ref, send_ref, keep_ref, g_ref):
    at = pl.program_id(0)
    embed = base_ref[...] + high_ref[...].astype(f32)
    unit = unit_ref[...]
    radial = jnp.sum(unit * embed, axis=-1, keepdims=True)
    p = ((embed - unit * radial) / radius_ref[...]).astype(bf16)
    p_ref[...] = p
    grad = jnp.dot(text_ref[...], p, preferred_element_type=f32)

    @pl.when(at == 0)
    def _():
        g_ref[...] = grad

    @pl.when(at > 0)
    def _():
        g_ref[...] += grad

    for core in range(2):

        @pl.when((at == pl.num_programs(0) - 1) & (c_ref[0] == core))
        def _():
            for x in range(n_x):
                for y in range(n_y):
                    for z in range(n_z):
                        mine = (((x * 2 + core) * n_z + z) * n_y + y) * piece
                        other = (((x * 2 + 1 - core) * n_z + z) * n_y + y) * piece
                        keep_ref[x * n_y + y, z, :piece, :] = g_ref[mine : mine + piece, :]
                        send_ref[x * n_y + y, z, :piece, :] = g_ref[other : other + piece, :].astype(bf16)


def finish(c, base, from_high, unit_rows, radius, text_t, n_x, n_z, n_y):
    rows, width = base.shape
    depth = text_t.shape[0]
    piece = depth // (n_x * 2 * n_z * n_y)
    tall = piece + -piece % 8
    steps = 2
    block = rows // steps
    by_row = pl.BlockSpec((block, width), lambda i: (i, 0))
    whole = pl.BlockSpec((n_x * n_y, n_z, tall, width), lambda i: (0, 0, 0, 0))
    return pl.pallas_call(
        functools.partial(finish_kernel, n_x, n_z, n_y, piece),
        grid=(steps,),
        out_shape=[
            jax.ShapeDtypeStruct((rows, width), bf16),
            jax.ShapeDtypeStruct((n_x * n_y, n_z, tall, width), bf16),
            jax.ShapeDtypeStruct((n_x * n_y, n_z, tall, width), f32),
        ],
        in_specs=[
            pl.BlockSpec(memory_space=pltpu.SMEM),
            by_row,
            by_row,
            by_row,
            pl.BlockSpec((block, 1), lambda i: (i, 0)),
            pl.BlockSpec((depth, block), lambda i: (0, i)),
        ],
        out_specs=[by_row, whole, whole],
        scratch_shapes=[pltpu.VMEM((depth, width), f32)],
        compiler_params=pltpu.CompilerParams(vmem_limit_bytes=40 << 20),
        cost_estimate=pl.CostEstimate(
            flops=2 * rows * depth * width, bytes_accessed=16 * rows * width + 6 * depth * width, transcendentals=rows
        ),
        name="finish",
    )(c.reshape(1), base, from_high, unit_rows, radius, text_t)


def slots_of(named, values, capacity):
    visits = named.shape[-1]
    order = jnp.arange(visits, dtype=jnp.int32)
    before = (order[:, None] < order[None, :]).astype(bf16)
    rank = jnp.dot(named.astype(bf16), before, preferred_element_type=f32)
    hit = named[..., None, :] & (rank[..., None, :] == jnp.arange(capacity, dtype=f32)[:, None])
    return jnp.sum(jnp.where(hit, values[..., None, :] + 1, 0), axis=-1) - 1


def gather_weight(proj, owners, blocks):
    n_x, n_c, n_h, n_l, n_y = (lax.axis_size(a) for a in ALL)
    x, c, zh, zl, y = (lax.axis_index(a) for a in ALL)
    rows, width = proj.shape
    n_z, n_xy = n_h * n_l, n_x * n_y
    listed = jnp.concatenate([owners.reshape(-1), blocks.reshape(-1)]).astype(bf16)
    entries = listed.shape[0]
    list_rows = -(-entries // width)
    listed = jnp.pad(listed, (0, list_rows * width - entries)).reshape(list_rows, width)
    piece = jnp.concatenate([proj.astype(bf16), listed])
    piece = jnp.pad(piece, ((0, -(rows + list_rows) % 8), (0, 0)))[None]
    column = [piece]
    for k in range(1, n_z):
        column.append(lax.ppermute(piece, COLUMN, [(i, i ^ k) for i in range(n_z)]))
    piece = jnp.concatenate(column)
    column_lists = piece[:, rows : rows + list_rows].reshape(n_z, -1)[:, :entries].astype(jnp.int32)
    flat = [piece]
    for k in range(1, n_xy):
        flat.append(lax.ppermute(piece, ("x", "y"), [(i, i ^ k) for i in range(n_xy)]))
    piece = jnp.concatenate(flat)
    other = lax.ppermute(piece, "c", SWAP)
    piece = jnp.concatenate([piece, other])
    xs, cs, zs, ys = jnp.arange(n_x), jnp.arange(n_c), jnp.arange(n_z), jnp.arange(n_y)
    far_c = (cs ^ c)[None, :, None, None]
    far_xy = ((xs[:, None] * n_y + ys[None, :]) ^ (x * n_y + y))[:, None, None, :]
    far_z = (zs ^ (zh * n_l + zl))[None, None, :, None]
    at = ((far_c * n_xy + far_xy) * n_z + far_z).reshape(-1)
    piece = jnp.take(piece, at, axis=0)
    lists = piece[:, rows : rows + list_rows].reshape(piece.shape[0], -1)[:, :entries].astype(jnp.int32)
    return piece[:, :rows].reshape(-1, width), column_lists, lists


def route(owners, column_lists, lists, capacity):
    n_blocks, hard = owners.shape
    visits = n_blocks * hard
    n_x, n_c, n_h, n_l, n_y = (lax.axis_size(a) for a in ALL)
    x, c, zh, zl, y = (lax.axis_index(a) for a in ALL)
    n_z = n_h * n_l
    xs, cs, ys = jnp.arange(n_x), jnp.arange(n_c), jnp.arange(n_y)
    z_at = zh * n_l + zl
    dest = (((xs[:, None, None] * n_c + cs[None, :, None]) * n_z) + z_at) * n_y + ys[None, None, :]
    dest = dest.reshape(-1, 1)
    me = ((x * n_c + c) * n_z + z_at) * n_y + y
    text_block = jnp.arange(visits, dtype=jnp.int32) // hard
    first = slots_of(owners.reshape(1, visits) == dest, text_block[None], capacity).reshape(-1)
    others = slots_of(column_lists[1:, None, :visits] == dest, text_block, capacity).reshape(n_z - 1, -1)
    table = lists.reshape(n_x, n_c, n_h, n_l, n_y, -1)
    table = jnp.where(zh == 0, table, jnp.flip(table, 2))
    table = jnp.where(zl == 0, table, jnp.flip(table, 3))
    table = table.transpose(2, 3, 0, 1, 4, 5).reshape(n_z, n_x * n_c * n_y, -1)
    tags = slots_of(table[:, :, :visits] == me, table[:, :, visits:], capacity).reshape(n_z, -1)
    return [first] + [others[k] for k in range(n_z - 1)], jnp.maximum(tags, 0)


def reduce_weight(send, keep, rows):
    n_xy, n_z, tall, width = send.shape
    other = lax.ppermute(send, "c", SWAP)
    total = (keep + other.astype(f32)).astype(bf16).reshape(n_xy, n_z * tall, width)
    total = lax.all_to_all(total, ("x", "y"), split_axis=0, concat_axis=0, tiled=True)
    total = jnp.sum(total.astype(f32), axis=0).reshape(n_z, tall, width).astype(bf16)
    total = lax.all_to_all(total, COLUMN, split_axis=0, concat_axis=0, tiled=True)
    return jnp.sum(total.astype(f32), axis=0)[:rows]


def step(text_feats, proj, first_moment, second_moment, owners, blocks, positives, bank):
    devices = lax.axis_size(ALL)
    plane = lax.axis_size(PLANE)
    rows_dev, _ = text_feats.shape
    text_blocks, hard = owners.shape
    tb = rows_dev // text_blocks
    visits = text_blocks * hard
    capacity = max(2, visits // devices + 1)

    text_low = lax.ppermute(text_feats, "zl", SWAP)
    half = rows_dev // 2 + tb
    highs, fars = [], []
    for part in (text_feats[:half], text_feats[half:]):
        highs.append(lax.ppermute(part, "zh", SWAP))
        fars.append(lax.ppermute(highs[-1], "zl", SWAP))
    text_high, text_far = jnp.concatenate(highs), jnp.concatenate(fars)
    weight_half, column_lists, lists = gather_weight(proj, owners, blocks)
    sources, tags = route(owners, column_lists, lists, capacity)
    texts = (text_feats, text_low, text_high, text_far)

    def exchange(rows):
        rows = rows.reshape(plane, capacity * tb, -1)
        rows = lax.all_to_all(rows, PLANE, split_axis=0, concat_axis=0, tiled=True)
        return rows.reshape(plane * capacity * tb, -1)

    picks, got, replies, partial = [], [], [], []
    for k in range(4):
        row_of = sources[k][:, None] * tb + jnp.arange(tb, dtype=jnp.int32)[None, :]
        row_of = jnp.where(sources[k][:, None] >= 0, row_of, -1).reshape(-1)
        pick = (row_of[:, None] == jnp.arange(rows_dev, dtype=jnp.int32)[None, :]).astype(bf16)
        sent = jnp.dot(pick, texts[k], preferred_element_type=f32).astype(bf16)
        picks.append(pick)
        got.append(exchange(sent))
    for k in range(4):
        replies += answer(got[k : k + 1], tags[k], weight_half, bank, tb)
    for k in range(4):
        reply = exchange(replies[k])
        partial.append(
            lax.dot_general(picks[k], reply, (((0,), (0,)), ((), ())), preferred_element_type=f32)
        )
    far_sum, high_sum = lax.optimization_barrier(partial[3].astype(bf16)), lax.optimization_barrier(partial[2])
    from_highs = []
    for part in (slice(0, half), slice(half, rows_dev)):
        from_far = lax.ppermute(far_sum[part], "zl", SWAP)
        both = (high_sum[part] + from_far.astype(f32)).astype(bf16)
        from_highs.append(lax.ppermute(both, "zh", SWAP))
    from_high = jnp.concatenate(from_highs)
    from_low = lax.ppermute(partial[1].astype(bf16), "zl", SWAP)
    projected = jnp.dot(text_feats, weight_half, preferred_element_type=f32)
    radius = jnp.sqrt(jnp.sum(projected * projected, axis=-1, keepdims=True) + norm_eps)
    unit_rows = projected / radius
    unit_half = unit_rows.astype(bf16)
    scores = logit_scale * jnp.dot(unit_half, bank.T, preferred_element_type=f32) + logit_bias
    columns = jnp.arange(bank.shape[0], dtype=jnp.int32)
    labels = jnp.where(columns[None, :] == positives[:, None], 1.0, -1.0).astype(f32)
    local_coef = (-labels * jax.nn.sigmoid(-labels * scores)).astype(bf16)
    local_grad = logit_scale * jnp.dot(local_coef, bank, preferred_element_type=f32)
    local_grad, unit_rows, radius = lax.optimization_barrier((local_grad, unit_rows, radius))

    base = local_grad + partial[0] + from_low.astype(f32)
    n_x, n_z, n_y = lax.axis_size("x"), lax.axis_size(COLUMN), lax.axis_size("y")
    proj_grad_rows, send, keep = finish(
        lax.axis_index("c").astype(jnp.int32), base, from_high, unit_rows, radius, text_feats.T, n_x, n_z, n_y
    )
    weight_grad = reduce_weight(send, keep, proj.shape[0])
    text_grad = lax.dot_general(
        proj_grad_rows, weight_half, (((1,), (1,)), ((), ())), preferred_element_type=f32
    ).astype(bf16)
    new_first = beta_one * first_moment + (1.0 - beta_one) * weight_grad
    new_second = beta_two * second_moment + (1.0 - beta_two) * weight_grad * weight_grad
    first_hat = new_first / (1.0 - beta_one**adam_step)
    second_hat = new_second / (1.0 - beta_two**adam_step)
    new_proj = proj - learn_rate * (first_hat / (jnp.sqrt(second_hat) + adam_eps) + decay_rate * proj)
    return (text_grad, new_proj, new_first, new_second)


def solution(mesh):
    n_gx, n_gy = mesh.shape["gx"], mesh.shape["gy"]
    fine = Mesh(mesh.devices.reshape(n_gx // 2, 2, 2, 2, n_gy // 4), ALL)
    rows = P(ALL, None)
    return jax.shard_map(
        step,
        mesh=fine,
        in_specs=(rows, rows, rows, rows, rows, rows, P(ALL), rows),
        out_specs=(rows, rows, rows, rows),
        check_vma=False,
    )
```
